128 devices in a mesh: replica: 16 (over z, x_hi, core), fsdp: 8 (over x_lo, y).
Axes of the slice: x: 4 (x_hi: 2, x_lo: 2; x = x_hi * 2 + x_lo), y: 4, z: 4, core: 2. Of those that a mesh axis runs over, the one named last changes fastest.
Arguments:
- weights: bfloat16 [4096, 14336], P(None, 'fsdp'), may hold values from -6 to 6
- head_vector: float32 [14336], P('fsdp'), may hold values from -6 to 6
- momentum: float32 [4096, 14336], P('replica', 'fsdp'), may hold values from -4 to 4
- batches: bfloat16 [1, 8192, 4096], P(None, ('replica', 'fsdp')), may hold values from -6 to 6
- pair_index: int32 [1, 4096, 2], P(None, 'replica'), may hold values from 0 to 511, as said below
- eval_rows: bfloat16 [1024, 4096], P(('replica', 'fsdp')), may hold values from -6 to 6
Outputs:
- momentum_out: float32 [4096, 14336], P('replica', 'fsdp')
- eval_rewards: float32 [1024], P(('replica', 'fsdp'))
The draws below stay inside these ranges and needn't reach their ends.
Inputs may be any that keep to these rules, and one draw needn't show every extreme that they name: `pair_index`: each pair names two different rows among its replica's 512 rows of that step; the first is the preferred one.
All inputs are finite; a program needn't handle non-finite values.
Results may differ from the reference program's by a relative error of at most 0.0038.
Values may be sent and summed in bfloat16 or wider, within the bound.
A program may use at most 192 MiB of HBM per device.

```python
import jax
import jax.numpy as jnp
from jax import lax

D = 4096
FF = 14336
BLOCK = 128
STEPS = 1
REP_TOKENS = 512
TOKENS_ALL = 8192
PAIRS_ALL = 4096
EVAL_ALL = 1024
N_REPLICA = 16


def draw_pair_index(key, part):
    first_key, second_key = jax.random.split(jax.random.fold_in(key, 17))
    chosen = jax.random.randint(first_key, (STEPS, PAIRS_ALL), 0, REP_TOKENS, dtype=jnp.int32)
    offset = jax.random.randint(second_key, (STEPS, PAIRS_ALL), 1, REP_TOKENS, dtype=jnp.int32)
    return jnp.stack([chosen, (chosen + offset) % REP_TOKENS], axis=-1)


def block_levels(stream_key, extent, pieces, low, high):
    def one(position, blocks):
        draws = jax.random.uniform(jax.random.fold_in(jax.random.fold_in(stream_key, 6), position), (blocks,), jnp.float32, low / len(pieces), high / len(pieces))
        return jnp.repeat(jnp.exp(draws), extent[position] // blocks).reshape((-1,) + (1,) * (len(extent) - position - 1))

    level = one(*pieces[0])
    for cut in pieces[1:]:
        level = level * one(*cut)
    return level


def noise(rng, dims, width, bound, shards=(), held_as=jnp.bfloat16):
    gain = block_levels(rng, dims, shards, -0.22, 0.18) if shards else 1.0
    result = jax.random.normal(rng, dims, jnp.float32) * width * gain
    return jnp.minimum(jnp.maximum(result, -bound), bound).astype(held_as)


def setup_inputs(seed: int = 0) -> dict:
    key_of = jax.random.split(jax.random.key(seed), 7)
    return {
        "weights": noise(key_of[0], (D, FF), 1.0, 6.0, ((1, 8),)),
        "head_vector": noise(key_of[1], (FF,), 1.0, 6.0, ((0, 8),), jnp.float32),
        "momentum": noise(key_of[2], (D, FF), 0.3, 4.0, ((0, 16), (1, 8)), jnp.float32),
        "batches": noise(key_of[3], (STEPS, TOKENS_ALL, D), 1.0, 6.0, ((1, 128),)),
        "pair_index": draw_pair_index(jax.random.fold_in(key_of[6], 71), 0),
        "eval_rows": noise(key_of[5], (EVAL_ALL, D), 1.0, 6.0, ((0, 128),)),
    }


inner_rate = 300.0
outer_rate = 0.7
outer_decay = 0.9
code_top = 448.0
epsilon = 1e-06

def forward(inputs, current, head_vector):
    hidden = jnp.dot(inputs, current, preferred_element_type=jnp.float32) * D ** (-0.5)
    squash = jax.nn.sigmoid(hidden)
    rewards = jnp.dot(hidden * squash, head_vector, precision=lax.Precision.HIGHEST) * FF ** (-0.5)
    return (hidden, squash, rewards)

def weight_grad(inputs, pair_local, current, head_vector):
    hidden, squash, rewards = forward(inputs, current, head_vector)
    chosen = pair_local[:, 0]
    rejected = pair_local[:, 1]
    pair_weight = jax.nn.sigmoid(rewards[rejected] - rewards[chosen])
    reward_grad = jnp.zeros_like(rewards).at[rejected].add(pair_weight).at[chosen].add(-pair_weight)
    head_scaled = head_vector * FF ** (-0.5)
    hidden_grad = (reward_grad[:, None] * head_scaled[None, :] * squash * (1.0 + hidden * (1.0 - squash))).astype(jnp.bfloat16)
    return lax.dot_general(inputs, hidden_grad, (((0,), (0,)), ((), ())), preferred_element_type=jnp.float32) * D ** (-0.5)

def quantize(matrix):
    blocks = matrix.reshape(matrix.shape[0] // BLOCK, BLOCK, matrix.shape[1])
    largest = lax.optimization_barrier(jnp.max(jnp.abs(blocks), axis=1))
    block_scale = ((largest + epsilon) / code_top).astype(jnp.bfloat16)
    coded = (blocks / block_scale.astype(jnp.float32)[:, None, :]).astype(jnp.bfloat16)
    return (coded.reshape(matrix.shape), block_scale)

def decode(coded, block_scale):
    blocks = coded.reshape(block_scale.shape[0], -1, coded.shape[1]).astype(jnp.float32)
    return (blocks * block_scale.astype(jnp.float32)[:, None, :]).reshape(coded.shape)

def local_delta(weights, head_vector, inputs_steps, pair_steps):
    accumulated = jnp.zeros(weights.shape, jnp.float32)
    current = weights
    for inner_step in range(STEPS):
        accumulated = accumulated + weight_grad(inputs_steps[inner_step], pair_steps[inner_step], current, head_vector)
        current = (weights.astype(jnp.float32) - inner_rate * accumulated).astype(jnp.bfloat16)
    return inner_rate * accumulated

def reference(weights, head_vector, momentum, batches, pair_index, eval_rows):
    replica_rows = batches.shape[1] // N_REPLICA
    replica_pairs = pair_index.shape[1] // N_REPLICA

    def one_replica(running, replica_index):
        inputs_steps = lax.dynamic_slice_in_dim(batches, replica_index * replica_rows, replica_rows, 1)
        pair_steps = lax.dynamic_slice_in_dim(pair_index, replica_index * replica_pairs, replica_pairs, 1)
        coded, block_scale = quantize(local_delta(weights, head_vector, inputs_steps, pair_steps))
        return (running + decode(coded, block_scale), None)
    scanned = lax.scan(one_replica, jnp.zeros(weights.shape, jnp.float32), jnp.arange(N_REPLICA, dtype=jnp.int32))
    pseudo = scanned[0] / N_REPLICA
    momentum_out = outer_decay * momentum + pseudo
    update = outer_rate * (pseudo + outer_decay * momentum_out)
    coded, block_scale = quantize(update)
    new_weights = (weights.astype(jnp.float32) - decode(coded, block_scale)).astype(jnp.bfloat16)
    eval_rewards = forward(eval_rows, new_weights, head_vector)[2]
    return (momentum_out, eval_rewards)
```

```python
import jax
import jax.numpy as jnp
from jax import lax
from jax.sharding import PartitionSpec as P

D = 4096
FF = 14336
N_REPLICA = 16

inner_rate = 300.0
outer_rate = 0.7
outer_decay = 0.9


def shards(weights, head_vector, momentum, batches, pair_index, eval_rows):
    head_scaled = head_vector * FF ** (-0.5)
    inputs = lax.all_gather(batches[0], "fsdp", axis=0, tiled=True)
    evals = lax.all_gather(eval_rows, "fsdp", axis=0, tiled=True)
    eval_slices = lax.all_to_all(evals, "replica", split_axis=1, concat_axis=0, tiled=True)

    hidden = jnp.dot(inputs, weights, preferred_element_type=jnp.float32) * D ** (-0.5)
    squash = jax.nn.sigmoid(hidden)
    partial_value = jnp.dot(hidden * squash, head_scaled, precision=lax.Precision.HIGHEST)
    rewards = lax.psum(partial_value, "fsdp")
    positions = jnp.arange(rewards.shape[0], dtype=jnp.int32)
    pair_local = pair_index[0]
    chosen = (pair_local[:, 0:1] == positions[None, :]).astype(jnp.float32)
    rejected = (pair_local[:, 1:2] == positions[None, :]).astype(jnp.float32)
    pair_table = rejected - chosen
    pair_gap = jnp.dot(pair_table, rewards, precision=lax.Precision.HIGHEST)
    pair_weight = jax.nn.sigmoid(pair_gap)
    reward_grad = jnp.dot(pair_weight, pair_table, precision=lax.Precision.HIGHEST)
    hidden_grad = (
        reward_grad[:, None] * head_scaled[None, :] * squash * (1.0 + hidden * (1.0 - squash))
    ).astype(jnp.bfloat16)
    scale = inner_rate * D ** (-0.5) / N_REPLICA
    deltas = (
        lax.dot_general(inputs, hidden_grad, (((0,), (0,)), ((), ())), preferred_element_type=jnp.float32) * scale
    ).astype(jnp.bfloat16)
    pseudo = lax.psum_scatter(deltas, "replica", scatter_dimension=0, tiled=True).astype(jnp.float32)
    momentum_out = outer_decay * momentum + pseudo
    update = (outer_rate * (pseudo + outer_decay * momentum_out)).astype(jnp.bfloat16)

    base = jnp.dot(evals, weights, preferred_element_type=jnp.float32)
    moved = jnp.dot(eval_slices, update, preferred_element_type=jnp.float32).astype(jnp.bfloat16)
    moved = lax.psum_scatter(moved, "replica", scatter_dimension=0, tiled=True).astype(jnp.float32)
    after = (base - moved) * D ** (-0.5)
    partial_eval = jnp.dot(after * jax.nn.sigmoid(after), head_scaled, precision=lax.Precision.HIGHEST)
    eval_rewards = lax.psum_scatter(partial_eval, "fsdp", scatter_dimension=0, tiled=True)
    return (momentum_out, eval_rewards)


def solution(mesh):
    return jax.shard_map(
        shards,
        mesh=mesh,
        in_specs=(
            P(None, "fsdp"),
            P("fsdp"),
            P("replica", "fsdp"),
            P(None, ("replica", "fsdp"), None),
            P(None, "replica", None),
            P(("replica", "fsdp"), None),
        ),
        out_specs=(P("replica", "fsdp"), P(("replica", "fsdp"))),
        check_vma=False,
    )
```

```python
import jax
import jax.numpy as jnp
from jax import lax
from jax.experimental import pallas as pl
from jax.experimental.pallas import tpu as pltpu
from jax.sharding import PartitionSpec as P

D = 4096
FF = 14336
N_REPLICA = 16

inner_rate = 300.0
outer_rate = 0.7
outer_decay = 0.9
HIGH = lax.Precision.HIGHEST
F32 = jnp.float32
BF16 = jnp.bfloat16
MESH = pl.DeviceIdType.MESH
TILE = 256


def rows_of(start, size):
    return pl.ds(pl.multiple_of(start, size), size)


def front_kernel(
    w_hbm, x_ref, e_ref, head_ref, pcol_ref, prow_ref,
    hg_ref, xt_ref, eg_ref, base_ref,
    w, xg, g, acc, rpart, rgrad,
    w_sem, x_send, x_recv, e_send, e_recv, r_send, r_recv,
):
    f = lax.axis_index("fsdp")
    xl, y = f // 4, f % 4
    up, down = (y + 1) % 4, (y + 3) % 4
    mine, other = xl * 4, (1 - xl) * 4

    load_w = pltpu.make_async_copy(w_hbm, w, w_sem)
    load_w.start()
    xg[rows_of(f * 64, 64), :] = x_ref[...]
    eg_ref[rows_of(f * 8, 8), :] = e_ref[...]

    barrier = pltpu.get_barrier_semaphore()
    for k in range(1, 8):
        pl.semaphore_signal(barrier, inc=1, device_id={"fsdp": (f + k) % 8}, device_id_type=MESH)
    pl.semaphore_wait(barrier, 7)

    def block(i, slot, peer, size=64, at=0):
        part = pl.ds(pl.multiple_of(slot * 64 + at, size), size)
        return pltpu.make_async_remote_copy(
            src_ref=xg.at[part, :], dst_ref=xg.at[part, :], send_sem=x_send.at[i], recv_sem=x_recv.at[i],
            device_id={"fsdp": peer}, device_id_type=MESH,
        )

    to_x = block(0, f, other + y)
    to_up = block(1, f, mine + up)
    to_down = block(2, f, mine + down)
    up_half = block(3, mine + down, mine + up, 32, 0)
    down_half = block(4, mine + up, mine + down, 32, 32)
    x_up = block(5, other + y, mine + up)
    x_down = block(6, other + y, mine + down)
    far_x = block(7, mine + (y + 2) % 4, other + y)
    for c in (to_x, to_up, to_down):
        c.start()
    to_up.wait_recv()
    up_half.start()
    to_down.wait_recv()
    down_half.start()
    to_x.wait_recv()
    x_up.start()
    x_down.start()

    def send_e(k):
        return pltpu.make_async_remote_copy(
            src_ref=e_ref, dst_ref=eg_ref.at[rows_of(f * 8, 8), :], send_sem=e_send.at[k], recv_sem=e_recv.at[k],
            device_id={"fsdp": (f + k) % 8}, device_id_type=MESH,
        )

    up_half.wait_recv()
    down_half.wait_recv()
    far_x.start()
    for k in range(1, 8):
        send_e(k).start()

    load_w.wait()

    def forward(group, column):
        acc[...] = jnp.zeros_like(acc)

        @pl.loop(0, 1792 // TILE)
        def _(n):
            cols = rows_of(n * TILE, TILE)
            h = jnp.dot(xg[rows_of(column * 64, 256), :], w[:, cols], preferred_element_type=F32) * D ** (-0.5)
            hs = head_ref[0:1, cols]
            sq = 1.0 / (1.0 + jnp.exp(-h))
            v = h * sq * hs
            acc[...] += v[:, :128] + v[:, 128:]
            g[group * 256 : group * 256 + 256, cols] = sq * (1.0 + h * (1.0 - sq)) * hs

        ones = jnp.ones((8, 128), F32)
        return lax.dot_general(ones, acc[...], (((1,), (1,)), ((), ())), precision=HIGH, preferred_element_type=F32)

    def turn(group, column):
        @pl.loop(0, D // TILE)
        def _(n):
            cols = rows_of(n * TILE, TILE)
            piece = xg[rows_of(column * 64, 256), cols]
            xt_ref[cols, group * 256 : group * 256 + 256] = piece.T

    first = forward(0, mine)
    turn(0, mine)
    x_up.wait_recv()
    x_down.wait_recv()
    far_x.wait_recv()
    second = forward(1, other)
    low = xl == 0
    row = jnp.concatenate([jnp.where(low, first, second), jnp.where(low, second, first)], axis=1)
    rpart[f] = row

    def send_r(k):
        return pltpu.make_async_remote_copy(
            src_ref=rpart.at[f], dst_ref=rpart.at[f], send_sem=r_send.at[k], recv_sem=r_recv.at[k],
            device_id={"fsdp": (f + k) % 8}, device_id_type=MESH,
        )

    for k in range(1, 8):
        send_r(k).start()
    turn(1, other)
    for k in range(1, 8):
        send_e(k).wait_recv()

    @pl.loop(0, 1792 // TILE)
    def _(n):
        cols = rows_of(n * TILE, TILE)
        base_ref[:, cols] = jnp.dot(eg_ref[...], w[:, cols], preferred_element_type=F32)

    for k in range(1, 8):
        send_r(k).wait_recv()
    rewards = jnp.sum(rpart[...], axis=0)
    at_col = lax.broadcasted_iota(jnp.int32, (256, 512), 1)
    table = (pcol_ref[:, 1:2] == at_col).astype(F32) - (pcol_ref[:, 0:1] == at_col).astype(F32)
    gap = lax.dot_general(table, rewards, (((1,), (1,)), ((), ())), precision=HIGH, preferred_element_type=F32)
    weight = 1.0 / (1.0 + jnp.exp(-gap))
    at_row = lax.broadcasted_iota(jnp.int32, (512, 256), 0)
    turned = (prow_ref[1:2, :] == at_row).astype(F32) - (prow_ref[0:1, :] == at_row).astype(F32)
    grad = jnp.dot(turned, weight, precision=HIGH, preferred_element_type=F32)
    rgrad[...] = jnp.broadcast_to(grad[:, 0:1], (512, 128))

    for group, column in ((0, mine), (1, other)):
        scale = jnp.tile(rgrad[rows_of(column * 64, 256), :], (1, 2))

        @pl.loop(0, 1792 // TILE)
        def _(n):
            cols = rows_of(n * TILE, TILE)
            at = slice(group * 256, group * 256 + 256)
            hg_ref[at, cols] = (scale * g[at, cols]).astype(BF16)

    for c in (to_x, to_up, to_down, up_half, down_half, x_up, x_down, far_x):
        c.wait_send()
    for k in range(1, 8):
        send_e(k).wait_send()
        send_r(k).wait_send()


def front(weights, inputs, evals, head_scaled, pairs):
    vmem = pl.BlockSpec(memory_space=pltpu.VMEM)
    return pl.pallas_call(
        front_kernel,
        out_shape=(
            jax.ShapeDtypeStruct((512, 1792), BF16),
            jax.ShapeDtypeStruct((4096, 512), BF16),
            jax.ShapeDtypeStruct((64, 4096), BF16),
            jax.ShapeDtypeStruct((64, 1792), F32),
        ),
        in_specs=[pl.BlockSpec(memory_space=pl.ANY)] + [vmem] * 5,
        out_specs=(vmem,) * 4,
        scratch_shapes=[
            pltpu.VMEM((4096, 1792), BF16),
            pltpu.VMEM((512, 4096), BF16),
            pltpu.VMEM((512, 1792), F32),
            pltpu.VMEM((256, 128), F32),
            pltpu.VMEM((8, 8, 512), F32),
            pltpu.VMEM((512, 128), F32),
            pltpu.SemaphoreType.DMA,
            pltpu.SemaphoreType.DMA((8,)),
            pltpu.SemaphoreType.DMA((8,)),
            pltpu.SemaphoreType.DMA((8,)),
            pltpu.SemaphoreType.DMA((8,)),
            pltpu.SemaphoreType.DMA((8,)),
            pltpu.SemaphoreType.DMA((8,)),
        ],
        compiler_params=pltpu.CompilerParams(collective_id=0, has_side_effects=True, vmem_limit_bytes=60 << 20),
    )(weights, inputs, evals, head_scaled, pairs, pairs.T)


def shards(weights, head_vector, momentum, batches, pair_index, eval_rows):
    head_scaled = head_vector * FF ** (-0.5)
    hidden_grad, turned, evals, base = front(weights, batches[0], eval_rows, head_scaled[None, :], pair_index[0])
    eval_slices = lax.all_to_all(evals, "replica", split_axis=1, concat_axis=0, tiled=True)
    scale = inner_rate * D ** (-0.5) / N_REPLICA
    deltas = (jnp.dot(turned, hidden_grad, preferred_element_type=jnp.float32) * scale).astype(jnp.bfloat16)
    pseudo = lax.psum_scatter(deltas, "replica", scatter_dimension=0, tiled=True).astype(jnp.float32)
    momentum_out = outer_decay * momentum + pseudo
    update = (outer_rate * (pseudo + outer_decay * momentum_out)).astype(jnp.bfloat16)

    moved = jnp.dot(eval_slices, update, preferred_element_type=jnp.float32).astype(jnp.bfloat16)
    moved = lax.psum_scatter(moved, "replica", scatter_dimension=0, tiled=True).astype(jnp.float32)
    after = (base - moved) * D ** (-0.5)
    partial_eval = jnp.dot(after * jax.nn.sigmoid(after), head_scaled, precision=lax.Precision.HIGHEST)
    eval_rewards = lax.psum_scatter(partial_eval, "fsdp", scatter_dimension=0, tiled=True)
    return (momentum_out, eval_rewards)


def solution(mesh):
    return jax.shard_map(
        shards,
        mesh=mesh,
        in_specs=(
            P(None, "fsdp"),
            P("fsdp"),
            P("replica", "fsdp"),
            P(None, ("replica", "fsdp"), None),
            P(None, "replica", None),
            P(("replica", "fsdp"), None),
        ),
        out_specs=(P("replica", "fsdp"), P(("replica", "fsdp"))),
        check_vma=False,
    )
```

```python
import jax
import jax.numpy as jnp
from jax import lax
from jax.experimental import pallas as pl
from jax.experimental.pallas import tpu as pltpu
from jax.sharding import PartitionSpec as P

D = 4096
FF = 14336
N_REPLICA = 16

inner_rate = 300.0
outer_rate = 0.7
outer_decay = 0.9
HIGH = lax.Precision.HIGHEST
F32 = jnp.float32
BF16 = jnp.bfloat16
MESH = pl.DeviceIdType.MESH
TILE = 256
CHUNKS = 7


def span(start, size):
    return pl.ds(pl.multiple_of(start, size), size)


def sigmoid(v):
    return 1.0 / (1.0 + jnp.exp(-v))


def round_kernel(
    w_hbm, mom_hbm, x_ref, e_ref, head_ref, pcol_ref, prow_ref,
    mout_hbm, eval_ref,
    w, mom, xg, g, acc, rpart, rgrad, eg, es, base,
    eo, xe, xt, xts, hg, cc, cown, m1, m1r, m2, m2r, u, hc, hown, h1, h1r, h2, h2r, hx, hxr, eacc, epart,
    load_sem, mout_sem, x_send, x_recv, e_send, e_recv, r_send, r_recv, s_send, s_recv,
    o_send, o_recv, g_send, g_recv, t_send, t_recv, hg_send, hg_recv, m_send, m_recv,
    u_send, u_recv, h_send, h_recv, f_send, f_recv,
):
    r = lax.axis_index("replica")
    f = lax.axis_index("fsdp")
    z, xh, c = r // 4, (r // 2) % 2, r % 2
    zx, q = z * 2 + xh, xh * 2 + c
    xl, y = f // 4, f % 4
    up, down = (y + 1) % 4, (y + 3) % 4
    mine, other = xl * 4, (1 - xl) * 4
    sib = z * 4 + xh * 2 + (1 - c)
    par = z * 4 + (1 - xh) * 2 + c
    z_up, z_down, z_far = (z + 1) % 4, (z + 3) % 4, (z + 2) % 4
    above, below = z_up * 4 + q, z_down * 4 + q

    def to_fsdp(src, dst, ss, rs, peer):
        return pltpu.make_async_remote_copy(
            src_ref=src, dst_ref=dst, send_sem=ss, recv_sem=rs, device_id={"fsdp": peer}, device_id_type=MESH)

    def to_rep(src, dst, ss, rs, peer):
        return pltpu.make_async_remote_copy(
            src_ref=src, dst_ref=dst, send_sem=ss, recv_sem=rs, device_id={"replica": peer}, device_id_type=MESH)

    load_w = pltpu.make_async_copy(w_hbm, w, load_sem.at[0])
    load_m = pltpu.make_async_copy(mom_hbm, mom, load_sem.at[1])
    load_w.start()
    load_m.start()

    barrier = pltpu.get_barrier_semaphore()
    for k in range(1, 8):
        pl.semaphore_signal(barrier, inc=1, device_id={"fsdp": (f + k) % 8}, device_id_type=MESH)
        pl.semaphore_signal(barrier, inc=1, device_id={"replica": ((zx + k) % 8) * 2 + c}, device_id_type=MESH)
    pl.semaphore_signal(barrier, inc=1, device_id={"replica": sib}, device_id_type=MESH)
    pl.semaphore_signal(
        barrier, inc=1, device_id={"replica": z * 4 + (1 - xh) * 2 + (1 - c)}, device_id_type=MESH)

    xg[span(f * 64, 64), :] = x_ref[...]
    for core in range(2):
        for zp in range(4):
            eo[core, zp] = x_ref[:, span(zp * 1024 + ((1 - xh) * 2 + core) * 256, 256)]
    eg[span(f * 8, 8), :] = e_ref[...]
    pl.semaphore_wait(barrier, 16)

    def block(i, slot, peer, size=64, at=0):
        part = pl.ds(pl.multiple_of(slot * 64 + at, size), size)
        return to_fsdp(xg.at[part, :], xg.at[part, :], x_send.at[i], x_recv.at[i], peer)

    to_x = block(0, f, other + y)
    to_up = block(1, f, mine + up)
    to_down = block(2, f, mine + down)
    up_half = block(3, mine + down, mine + up, 32, 0)
    down_half = block(4, mine + up, mine + down, 32, 32)
    x_up = block(5, other + y, mine + up)
    x_down = block(6, other + y, mine + down)
    far_x = block(7, mine + (y + 2) % 4, other + y)
    main = (to_x, to_up, to_down, up_half, down_half, x_up, x_down, far_x)

    def extra(i, ref, peer):
        return to_fsdp(ref, ref, g_send.at[i], g_recv.at[i], peer)

    ex_x = extra(0, xe.at[f], other + y)
    ex_up = extra(1, xe.at[f], mine + up)
    ex_down = extra(2, xe.at[f], mine + down)
    ex_up_half = extra(3, xe.at[mine + down, 0], mine + up)
    ex_down_half = extra(4, xe.at[mine + up, 1], mine + down)
    ex_x_up = extra(5, xe.at[other + y], mine + up)
    ex_x_down = extra(6, xe.at[other + y], mine + down)
    ex_far = extra(7, xe.at[mine + (y + 2) % 4], other + y)
    extras = (ex_x, ex_up, ex_down, ex_up_half, ex_down_half, ex_x_up, ex_x_down, ex_far)

    def over(core):
        peer = z * 4 + (1 - xh) * 2 + core
        return to_rep(eo.at[core], xe.at[f, c], o_send.at[core], o_recv.at[c], peer)

    def over_from(core):
        peer = z * 4 + (1 - xh) * 2 + core
        return to_rep(eo.at[core], xe.at[f, core], o_send.at[core], o_recv.at[core], peer)

    for copy in (to_x, to_up, to_down):
        copy.start()
    over(0).start()
    over(1).start()
    to_up.wait_recv()
    up_half.start()
    to_down.wait_recv()
    down_half.start()
    to_x.wait_recv()
    x_up.start()
    x_down.start()

    def send_e(k):
        return to_fsdp(e_ref, eg.at[span(f * 8, 8), :], e_send.at[k], e_recv.at[k], (f + k) % 8)

    up_half.wait_recv()
    down_half.wait_recv()
    far_x.start()
    for k in range(1, 8):
        send_e(k).start()
    over_from(0).wait_recv()
    over_from(1).wait_recv()
    ex_x.start()
    ex_up.start()
    ex_down.start()

    load_w.wait()

    def forward(group, column):
        acc[...] = jnp.zeros_like(acc)

        @pl.loop(0, CHUNKS)
        def _(n):
            cols = span(n * TILE, TILE)
            h = jnp.dot(xg[span(column * 64, 256), :], w[:, cols], preferred_element_type=F32) * D ** (-0.5)
            hs = head_ref[0:1, cols]
            sq = sigmoid(h)
            v = h * sq * hs
            acc[...] += v[:, :128] + v[:, 128:]
            g[group * 256 : group * 256 + 256, cols] = sq * (1.0 + h * (1.0 - sq)) * hs

        ones = jnp.ones((8, 128), F32)
        return lax.dot_general(ones, acc[...], (((1,), (1,)), ((), ())), precision=HIGH, preferred_element_type=F32)

    def turn(group, column):
        @pl.loop(0, 4)
        def _(zp):
            at = slice(group * 256, group * 256 + 256)
            xt[zp, :, at] = xg[span(column * 64, 256), span(zp * 1024 + q * 256, 256)].T
            xts[zp, :, at] = xg[span(column * 64, 256), span(zp * 1024 + (xh * 2 + 1 - c) * 256, 256)].T

    def turn_extra(group, column):
        @pl.loop(0, 4)
        def _(zp):
            for core in range(2):
                at = slice(1024 + core * 512 + group * 256, 1024 + core * 512 + group * 256 + 256)
                xt[zp, :, at] = xe[pl.ds(column, 4), core, zp].reshape(256, 256).T

    first = forward(0, mine)
    turn(0, mine)
    x_up.wait_recv()
    x_down.wait_recv()
    far_x.wait_recv()
    second = forward(1, other)
    low = xl == 0
    rpart[f] = jnp.concatenate([jnp.where(low, first, second), jnp.where(low, second, first)], axis=1)

    def send_r(k):
        return to_fsdp(rpart.at[f], rpart.at[f], r_send.at[k], r_recv.at[k], (f + k) % 8)

    for k in range(1, 8):
        send_r(k).start()
    ex_up.wait_recv()
    ex_up_half.start()
    ex_down.wait_recv()
    ex_down_half.start()
    ex_x.wait_recv()
    ex_x_up.start()
    ex_x_down.start()
    turn(1, other)
    send_t = to_rep(xts, xt.at[:, :, 512:1024], t_send, t_recv, sib)
    send_t.start()

    for k in range(1, 8):
        send_r(k).wait_recv()
    rewards = jnp.sum(rpart[...], axis=0)
    at_col = lax.broadcasted_iota(jnp.int32, (256, 512), 1)
    table = (pcol_ref[:, 1:2] == at_col).astype(F32) - (pcol_ref[:, 0:1] == at_col).astype(F32)
    gap = lax.dot_general(table, rewards, (((1,), (1,)), ((), ())), precision=HIGH, preferred_element_type=F32)
    weight = sigmoid(gap)
    at_row = lax.broadcasted_iota(jnp.int32, (512, 256), 0)
    turned = (prow_ref[1:2, :] == at_row).astype(F32) - (prow_ref[0:1, :] == at_row).astype(F32)
    grad = jnp.dot(turned, weight, precision=HIGH, preferred_element_type=F32)
    rgrad[...] = jnp.broadcast_to(grad[:, 0:1], (512, 128))

    def hg_sib(k):
        return to_rep(hg.at[k, 0], hg.at[k, 1], hg_send.at[k, 0], hg_recv.at[k, 0], sib)

    def hg_par(k):
        return to_rep(hg.at[k, 0], hg.at[k, 2 + c], hg_send.at[k, 1], hg_recv.at[k, 1], par)

    def hg_fwd(k):
        return to_rep(hg.at[k, 2 + c], hg.at[k, 2 + c], hg_send.at[k, 2], hg_recv.at[k, 2], sib)

    @pl.loop(0, CHUNKS)
    def _(k):
        cols = span(k * TILE, TILE)
        for group, column in ((0, mine), (1, other)):
            scale = jnp.tile(rgrad[span(column * 64, 256), :], (1, 2))
            at = slice(group * 256, group * 256 + 256)
            hg[k, 0, at, :] = (scale * g[at, cols]).astype(BF16)
        hg_par(k).start()
        hg_sib(k).start()

    ex_up_half.wait_recv()
    ex_down_half.wait_recv()
    ex_far.start()
    for k in range(1, 8):
        send_e(k).wait_recv()

    def send_s(k):
        peer = (zx + k) % 8
        return to_rep(eg.at[:, span(peer * 512, 512)], es.at[zx], s_send.at[k], s_recv.at[k], peer * 2 + c)

    for k in range(1, 8):
        send_s(k).start()
    es[zx] = eg[:, span(zx * 512, 512)]

    @pl.loop(0, CHUNKS)
    def _(n):
        cols = span(n * TILE, TILE)
        base[:, cols] = jnp.dot(eg[...], w[:, cols], preferred_element_type=F32)

    turn_extra(0, mine)
    ex_x_up.wait_recv()
    ex_x_down.wait_recv()
    ex_far.wait_recv()
    turn_extra(1, other)
    send_t.wait_recv()
    for k in range(1, 8):
        send_s(k).wait_recv()
    load_m.wait()
    eacc[...] = jnp.zeros_like(eacc)

    def reduce_copy(k, i, bufs, send, recv):
        src, dst, j = (bufs[0], bufs[1], i) if i < 2 else (bufs[2], bufs[3], i - 2)
        peer = below if i in (0, 2, 3) else above
        return to_rep(src.at[k, j], dst.at[k, j], send.at[k, i], recv.at[k, i], peer)

    def m_copy(k, i):
        return reduce_copy(k, i, (m1, m1r, m2, m2r), m_send, m_recv)

    def h_copy(k, i):
        return reduce_copy(k, i, (h1, h1r, h2, h2r), h_send, h_recv)

    def send_u(k):
        return to_rep(u.at[k, c], u.at[k, c], u_send.at[k], u_recv.at[k], sib)

    def send_hx(k):
        return to_rep(hx.at[k], hxr.at[k], h_send.at[k, 6], h_recv.at[k, 6], par)

    def mout_copy(k):
        cols = span(k * TILE, TILE)
        return pltpu.make_async_copy(mom.at[:, cols], mout_hbm.at[:, cols], mout_sem.at[k])

    grad_scale = inner_rate * D ** (-0.5) / N_REPLICA

    def stage(step, lag):
        k = step - lag
        return k, pl.when(jnp.logical_and(k >= 0, k < CHUNKS))

    @pl.loop(0, CHUNKS + 6)
    def _(step):
        k0, on0 = stage(step, 0)

        @on0
        def _():
            hg_par(k0).wait_recv()
            hg_fwd(k0).start()

        k1, on1 = stage(step, 1)

        @on1
        def _():
            m_copy(k1, 0).wait_recv()
            m2[k1, 0] = (cc[z_down, 0:128] + m1r[k1, 0].astype(F32)).astype(BF16)
            m_copy(k1, 2).start()
            m_copy(k1, 1).wait_recv()
            m2[k1, 3] = (cc[z_up, 128:256] + m1r[k1, 1].astype(F32)).astype(BF16)
            m_copy(k1, 5).start()

        k2, on2 = stage(step, 2)

        @on2
        def _():
            for i in range(2, 6):
                m_copy(k2, i).wait_recv()
            cols = span(k2 * TILE, TILE)
            for half, one, two in ((0, 0, 2), (1, 1, 3)):
                at = slice(half * 128, half * 128 + 128)
                pseudo = cown[k2, at] + (m2r[k2, one].astype(F32) + m2r[k2, two].astype(F32))
                new = outer_decay * mom[at, cols] + pseudo
                mom[at, cols] = new
                u[k2, c, at] = (outer_rate * (pseudo + outer_decay * new)).astype(BF16)
            send_u(k2).start()
            mout_copy(k2).start()

        k6, on6 = stage(step, 6)

        @on6
        def _():
            send_hx(k6).wait_recv()
            cols = span(k6 * TILE, TILE)
            moved = hown[k6, xh] + hxr[k6].astype(F32)
            after = (base[:, cols] - moved) * D ** (-0.5)
            v = after * sigmoid(after) * head_ref[0:1, cols]
            eacc[...] += v[:, :128] + v[:, 128:]

        k5, on5 = stage(step, 5)

        @on5
        def _():
            for i in range(2, 6):
                h_copy(k5, i).wait_recv()
            hown[k5, 0] += h2r[k5, 0].astype(F32) + h2r[k5, 2].astype(F32)
            hown[k5, 1] += h2r[k5, 1].astype(F32) + h2r[k5, 3].astype(F32)
            hx[k5] = hown[k5, 1 - xh].astype(BF16)
            send_hx(k5).start()

        k4, on4 = stage(step, 4)

        @on4
        def _():
            h_copy(k4, 0).wait_recv()
            h2[k4, 0] = (hc[z_down * 2] + h1r[k4, 0].astype(F32)).astype(BF16)
            h_copy(k4, 2).start()
            h_copy(k4, 1).wait_recv()
            h2[k4, 3] = (hc[z_up * 2 + 1] + h1r[k4, 1].astype(F32)).astype(BF16)
            h_copy(k4, 5).start()

        k3, on3 = stage(step, 3)

        @on3
        def _():
            send_u(k3).wait_recv()
            hc[...] = jnp.dot(
                es[...].reshape(512, 512), u[k3].reshape(512, TILE), preferred_element_type=F32
            ).reshape(8, 64, TILE)
            h1[k3, 0] = hc[z_far * 2].astype(BF16)
            h_copy(k3, 0).start()
            h1[k3, 1] = hc[z_far * 2 + 1].astype(BF16)
            h_copy(k3, 1).start()
            h2[k3, 1] = hc[z_down * 2 + 1].astype(BF16)
            h_copy(k3, 3).start()
            h2[k3, 2] = hc[z_up * 2].astype(BF16)
            h_copy(k3, 4).start()
            hown[k3, 0] = hc[z * 2]
            hown[k3, 1] = hc[z * 2 + 1]

        @on0
        def _():
            hg_sib(k0).wait_recv()
            hg_fwd_in = to_rep(
                hg.at[k0, 3 - c], hg.at[k0, 3 - c], hg_send.at[k0, 2], hg_recv.at[k0, 2], sib)
            hg_fwd_in.wait_recv()
            cc[...] = (
                jnp.dot(xt[...].reshape(1024, 2048), hg[k0].reshape(2048, TILE), preferred_element_type=F32)
                * grad_scale
            ).reshape(4, 256, TILE)
            m1[k0, 0] = cc[z_far, 0:128].astype(BF16)
            m_copy(k0, 0).start()
            m1[k0, 1] = cc[z_far, 128:256].astype(BF16)
            m_copy(k0, 1).start()
            m2[k0, 1] = cc[z_down, 128:256].astype(BF16)
            m_copy(k0, 3).start()
            m2[k0, 2] = cc[z_up, 0:128].astype(BF16)
            m_copy(k0, 4).start()
            cown[k0] = cc[z]

    def send_f(k):
        peer = (f + k) % 8
        return to_fsdp(eacc.at[span(peer * 8, 8), :], epart.at[f], f_send.at[k], f_recv.at[k], peer)

    for k in range(1, 8):
        send_f(k).start()
    epart[f] = eacc[span(f * 8, 8), :]

    @pl.loop(0, CHUNKS)
    def _(k):
        mout_copy(k).wait()
        for i in range(6):
            m_copy(k, i).wait_send()
            h_copy(k, i).wait_send()
        for copy in (hg_sib(k), hg_par(k), hg_fwd(k), send_u(k), send_hx(k)):
            copy.wait_send()

    for copy in main + extras + (send_t, over(0), over(1)):
        copy.wait_send()
    for k in range(1, 8):
        send_e(k).wait_send()
        send_r(k).wait_send()
        send_s(k).wait_send()
    for k in range(1, 8):
        send_f(k).wait_recv()
    eval_ref[...] = jnp.sum(jnp.sum(epart[...], axis=0), axis=1, keepdims=True)
    for k in range(1, 8):
        send_f(k).wait_send()


def whole_round(weights, momentum, inputs, evals, head_scaled, pairs):
    vmem = pl.BlockSpec(memory_space=pltpu.VMEM)
    hbm = pl.BlockSpec(memory_space=pl.ANY)
    dma = pltpu.SemaphoreType.DMA
    return pl.pallas_call(
        round_kernel,
        out_shape=(jax.ShapeDtypeStruct((256, 1792), F32), jax.ShapeDtypeStruct((8, 1), F32)),
        in_specs=[hbm, hbm] + [vmem] * 5,
        out_specs=(hbm, vmem),
        scratch_shapes=[
            pltpu.VMEM((4096, 1792), BF16),
            pltpu.VMEM((256, 1792), F32),
            pltpu.VMEM((512, 4096), BF16),
            pltpu.VMEM((512, 1792), F32),
            pltpu.VMEM((256, 128), F32),
            pltpu.VMEM((8, 8, 512), F32),
            pltpu.VMEM((512, 128), F32),
            pltpu.VMEM((64, 4096), BF16),
            pltpu.VMEM((8, 64, 512), BF16),
            pltpu.VMEM((64, 1792), F32),
            pltpu.VMEM((2, 4, 64, 256), BF16),
            pltpu.VMEM((8, 2, 4, 64, 256), BF16),
            pltpu.VMEM((4, 256, 2048), BF16),
            pltpu.VMEM((4, 256, 512), BF16),
            pltpu.VMEM((CHUNKS, 4, 512, TILE), BF16),
            pltpu.VMEM((4, 256, TILE), F32),
            pltpu.VMEM((CHUNKS, 256, TILE), F32),
            pltpu.VMEM((CHUNKS, 2, 128, TILE), BF16),
            pltpu.VMEM((CHUNKS, 2, 128, TILE), BF16),
            pltpu.VMEM((CHUNKS, 4, 128, TILE), BF16),
            pltpu.VMEM((CHUNKS, 4, 128, TILE), BF16),
            pltpu.VMEM((CHUNKS, 2, 256, TILE), BF16),
            pltpu.VMEM((8, 64, TILE), F32),
            pltpu.VMEM((CHUNKS, 2, 64, TILE), F32),
            pltpu.VMEM((CHUNKS, 2, 64, TILE), BF16),
            pltpu.VMEM((CHUNKS, 2, 64, TILE), BF16),
            pltpu.VMEM((CHUNKS, 4, 64, TILE), BF16),
            pltpu.VMEM((CHUNKS, 4, 64, TILE), BF16),
            pltpu.VMEM((CHUNKS, 64, TILE), BF16),
            pltpu.VMEM((CHUNKS, 64, TILE), BF16),
            pltpu.VMEM((64, 128), F32),
            pltpu.VMEM((8, 8, 128), F32),
            dma((2,)),
            dma((CHUNKS,)),
            dma((8,)), dma((8,)),
            dma((8,)), dma((8,)),
            dma((8,)), dma((8,)),
            dma((8,)), dma((8,)),
            dma((2,)), dma((2,)),
            dma((8,)), dma((8,)),
            dma, dma,
            dma((CHUNKS, 3)), dma((CHUNKS, 3)),
            dma((CHUNKS, 6)), dma((CHUNKS, 6)),
            dma((CHUNKS,)), dma((CHUNKS,)),
            dma((CHUNKS, 7)), dma((CHUNKS, 7)),
            dma((8,)), dma((8,)),
        ],
        compiler_params=pltpu.CompilerParams(collective_id=0, has_side_effects=True, vmem_limit_bytes=63 << 20),
    )(weights, momentum, inputs, evals, head_scaled, pairs, pairs.T)


def shards(weights, head_vector, momentum, batches, pair_index, eval_rows):
    head_scaled = head_vector * FF ** (-0.5)
    momentum_out, eval_rewards = whole_round(
        weights, momentum, batches[0], eval_rows, head_scaled[None, :], pair_index[0])
    return (momentum_out, eval_rewards[:, 0])


def solution(mesh):
    return jax.shard_map(
        shards,
        mesh=mesh,
        in_specs=(
            P(None, "fsdp"),
            P("fsdp"),
            P("replica", "fsdp"),
            P(None, ("replica", "fsdp"), None),
            P(None, "replica", None),
            P(("replica", "fsdp"), None),
        ),
        out_specs=(P("replica", "fsdp"), P(("replica", "fsdp"))),
        check_vma=False,
    )
```

```python
import jax
import jax.numpy as jnp
from jax import lax
from jax.experimental import pallas as pl
from jax.experimental.pallas import tpu as pltpu
from jax.sharding import PartitionSpec as P

D = 4096
FF = 14336
N_REPLICA = 16

inner_rate = 300.0
outer_rate = 0.7
outer_decay = 0.9
HIGH = lax.Precision.HIGHEST
F32 = jnp.float32
BF16 = jnp.bfloat16
MESH = pl.DeviceIdType.MESH
TILE = 256
CHUNKS = 7
AHEAD = 2
LAGS = (0, 1, 2, 3, 4, 5, 6)


def span(start, size):
    return pl.ds(pl.multiple_of(start, size), size)


def sigmoid(v):
    return 1.0 / (1.0 + jnp.exp(-v))


def round_kernel(
    w_hbm, mom_hbm, x_ref, e_ref, head_ref, pair_ref,
    mout_hbm, eval_ref,
    w, mom, xg, acc, rpart, rgrad, eg, es,
    eo, xe, xt, xts, hg, rcol, hgs, cc, cown, cmid, m1, m1r, m2, m2r, u, hc, hown, h1, h1r, h2, h2r, hx, hxr, eacc, epart,
    load_sem, mout_sem, x_send, x_recv, e_send, e_recv, r_send, r_recv, s_send, s_recv,
    o_send, o_recv, g_send, g_recv, t_send, t_recv, hg_send, hg_recv, q_send, q_recv, m_send, m_recv,
    u_send, u_recv, h_send, h_recv, f_send, f_recv,
):
    r = lax.axis_index("replica")
    f = lax.axis_index("fsdp")
    z, xh, c = r // 4, (r // 2) % 2, r % 2
    zx, q = z * 2 + xh, xh * 2 + c
    xl, y = f // 4, f % 4
    up, down = (y + 1) % 4, (y + 3) % 4
    mine, other = xl * 4, (1 - xl) * 4
    sib = z * 4 + xh * 2 + (1 - c)
    par = z * 4 + (1 - xh) * 2 + c
    z_up, z_down, z_far = (z + 1) % 4, (z + 3) % 4, (z + 2) % 4
    above, below = z_up * 4 + q, z_down * 4 + q

    def to_fsdp(src, dst, ss, rs, peer):
        return pltpu.make_async_remote_copy(
            src_ref=src, dst_ref=dst, send_sem=ss, recv_sem=rs, device_id={"fsdp": peer}, device_id_type=MESH)

    def to_rep(src, dst, ss, rs, peer):
        return pltpu.make_async_remote_copy(
            src_ref=src, dst_ref=dst, send_sem=ss, recv_sem=rs, device_id={"replica": peer}, device_id_type=MESH)

    load_w = pltpu.make_async_copy(w_hbm, w, load_sem.at[0])
    load_m = pltpu.make_async_copy(mom_hbm, mom, load_sem.at[1])
    load_w.start()
    load_m.start()

    barrier = pltpu.get_barrier_semaphore()
    for k in range(1, 8):
        pl.semaphore_signal(barrier, inc=1, device_id={"fsdp": (f + k) % 8}, device_id_type=MESH)
        pl.semaphore_signal(barrier, inc=1, device_id={"replica": ((zx + k) % 8) * 2 + c}, device_id_type=MESH)
    pl.semaphore_signal(barrier, inc=1, device_id={"replica": sib}, device_id_type=MESH)
    pl.semaphore_signal(
        barrier, inc=1, device_id={"replica": z * 4 + (1 - xh) * 2 + (1 - c)}, device_id_type=MESH)
    for core in range(2):
        pl.semaphore_signal(
            barrier, inc=1, device_id={"replica": z * 4 + (1 - xh) * 2 + core, "fsdp": other + y},
            device_id_type=MESH)

    xg[span(f * 64, 64), :] = x_ref[...]
    for core in range(2):
        for zp in range(4):
            eo[core, zp] = x_ref[:, span(zp * 1024 + ((1 - xh) * 2 + core) * 256, 256)]
    eg[span(f * 8, 8), :] = e_ref[...]
    pl.semaphore_wait(barrier, 18)

    def block(i, slot, peer, size=64, at=0):
        part = pl.ds(pl.multiple_of(slot * 64 + at, size), size)
        return to_fsdp(xg.at[part, :], xg.at[part, :], x_send.at[i], x_recv.at[i], peer)

    to_x = block(0, f, other + y)
    to_up = block(1, f, mine + up)
    to_down = block(2, f, mine + down)
    up_half = block(3, mine + down, mine + up, 32, 0)
    down_half = block(4, mine + up, mine + down, 32, 32)
    x_up = block(5, other + y, mine + up)
    x_down = block(6, other + y, mine + down)
    far_x = block(7, mine + (y + 2) % 4, other + y)
    main = (to_x, to_up, to_down, up_half, down_half, x_up, x_down, far_x)

    def extra(i, ref, peer):
        return to_fsdp(ref, ref, g_send.at[i], g_recv.at[i], peer)

    ex_first = (
        extra(0, xe.at[f], mine + up),
        extra(1, xe.at[f], mine + down),
        extra(2, xe.at[other + y], mine + up),
        extra(3, xe.at[other + y], mine + down),
    )
    ex_second = (
        extra(4, xe.at[mine + down, 0], mine + up),
        extra(5, xe.at[mine + up, 1], mine + down),
        extra(6, xe.at[other + down, 0], mine + up),
        extra(7, xe.at[other + up, 1], mine + down),
    )
    extras = ex_first + ex_second

    def over(core, i):
        return pltpu.make_async_remote_copy(
            src_ref=eo.at[core], dst_ref=xe.at[f, c], send_sem=o_send.at[core, i], recv_sem=o_recv.at[c, i],
            device_id={"replica": z * 4 + (1 - xh) * 2 + core, "fsdp": (mine if i == 0 else other) + y},
            device_id_type=MESH)

    def over_in(core, i):
        return pltpu.make_async_remote_copy(
            src_ref=eo.at[core], dst_ref=xe.at[(mine if i == 0 else other) + y, core], send_sem=o_send.at[core, i],
            recv_sem=o_recv.at[core, i],
            device_id={"replica": z * 4 + (1 - xh) * 2 + core, "fsdp": (mine if i == 0 else other) + y},
            device_id_type=MESH)

    overs = tuple((core, i) for core in range(2) for i in range(2))

    for copy in (to_x, to_up, to_down):
        copy.start()

    def send_e(k):
        return to_fsdp(e_ref, eg.at[span(f * 8, 8), :], e_send.at[k], e_recv.at[k], (f + k) % 8)

    to_up.wait_recv()
    up_half.start()
    to_down.wait_recv()
    down_half.start()
    to_x.wait_recv()
    for core, i in overs:
        over(core, i).start()
    up_half.wait_recv()
    down_half.wait_recv()
    far_x.start()
    x_up.start()
    x_down.start()

    load_w.wait()

    def hg_copy(k, group, i, src, dst, peer):
        at = slice(group * 256, group * 256 + 256)
        return to_rep(
            hg.at[k, src, at], hg.at[k, dst, at], hg_send.at[k, group, i], hg_recv.at[k, group, i], peer)

    def hg_sib(k, group):
        return hg_copy(k, group, 0, 0, 1, sib)

    def hg_par(k, group):
        return hg_copy(k, group, 1, 0, 2 + c, par)

    def hg_fwd(k, group):
        return hg_copy(k, group, 2, 2 + c, 2 + c, sib)

    def hg_fwd_in(k, group):
        return hg_copy(k, group, 2, 3 - c, 3 - c, sib)

    def forward(group, column):
        acc[...] = jnp.zeros_like(acc)

        @pl.loop(0, CHUNKS)
        def _(n):
            cols = span(n * TILE, TILE)
            h = jnp.dot(xg[span(column * 64, 256), :], w[:, cols], preferred_element_type=F32) * D ** (-0.5)
            hs = head_ref[0:1, cols]
            sq = sigmoid(h)
            v = h * sq * hs
            acc[...] += v[:, :128] + v[:, 128:]
            hg[n, 0, group * 256 : group * 256 + 256, :] = (sq * (1.0 + h * (1.0 - sq)) * hs).astype(BF16)
            hg_sib(n, group).start()

            if group == 1:

                @pl.when(n < AHEAD)
                def _():
                    hg_par(n, group).start()

        ones = jnp.ones((8, 128), F32)
        return lax.dot_general(ones, acc[...], (((1,), (1,)), ((), ())), precision=HIGH, preferred_element_type=F32)

    def turn(group, column):
        @pl.loop(0, 4)
        def _(zp):
            at = slice(group * 256, group * 256 + 256)
            xt[zp, :, at] = xg[span(column * 64, 256), span(zp * 1024 + q * 256, 256)].T
            xts[zp, :, at] = xg[span(column * 64, 256), span(zp * 1024 + (xh * 2 + 1 - c) * 256, 256)].T

    def turn_extra(group, column):
        @pl.loop(0, 4)
        def _(zp):
            for core in range(2):
                at = slice(1024 + core * 512 + group * 256, 1024 + core * 512 + group * 256 + 256)
                xt[zp, :, at] = xe[pl.ds(column, 4), core, zp].reshape(256, 256).T

    first = forward(0, mine)
    turn(0, mine)
    x_up.wait_recv()
    x_down.wait_recv()
    far_x.wait_recv()
    for core, i in overs:
        over_in(core, i).wait_recv()
    for copy in ex_first:
        copy.start()

    @pl.loop(0, 2)
    def _(k):
        hg_par(k, 0).start()

    for k in range(1, 8):
        send_e(k).start()
    second = forward(1, other)
    low = xl == 0
    rpart[f] = jnp.concatenate([jnp.where(low, first, second), jnp.where(low, second, first)], axis=1)

    def send_r(k):
        return to_fsdp(rpart.at[f], rpart.at[f], r_send.at[k], r_recv.at[k], (f + k) % 8)

    for k in range(1, 8):
        send_r(k).start()
    ex_first[0].wait_recv()
    ex_second[0].start()
    ex_first[1].wait_recv()
    ex_second[1].start()
    ex_first[2].wait_recv()
    ex_second[2].start()
    ex_first[3].wait_recv()
    ex_second[3].start()
    turn(1, other)
    send_t = to_rep(xts, xt.at[:, :, 512:1024], t_send, t_recv, sib)
    send_t.start()

    for k in range(1, 8):
        send_r(k).wait_recv()
    rewards = jnp.sum(rpart[...], axis=0)
    at_row = lax.broadcasted_iota(jnp.int32, (512, 256), 0)
    turned = (pair_ref[1:2, :] == at_row).astype(F32) - (pair_ref[0:1, :] == at_row).astype(F32)
    weight = sigmoid(jnp.dot(rewards, turned, precision=HIGH, preferred_element_type=F32))
    grad = lax.dot_general(weight, turned, (((1,), (1,)), ((), ())), precision=HIGH, preferred_element_type=F32)
    rgrad[0] = jnp.where(low, grad, jnp.concatenate([grad[:, 256:], grad[:, :256]], axis=1))

    def send_q(i):
        peer = (sib, z * 4 + (1 - xh) * 2, z * 4 + (1 - xh) * 2 + 1)[i]
        return to_rep(rgrad.at[0], rgrad.at[1 if i == 0 else 2 + c], q_send.at[i], q_recv.at[0 if i == 0 else 1 + c], peer)

    def recv_q(i):
        return to_rep(rgrad.at[0], rgrad.at[1 + i], q_send.at[i], q_recv.at[i], sib)

    for i in range(3):
        send_q(i).start()

    hg_par(2, 0).start()
    hg_par(2, 1).start()
    for k in range(1, 8):
        send_e(k).wait_recv()

    def send_s(k):
        peer = (zx + k) % 8
        return to_rep(eg.at[:, span(peer * 512, 512)], es.at[zx], s_send.at[k], s_recv.at[k], peer * 2 + c)

    for k in range(1, 8):
        send_s(k).start()
    es[zx] = eg[:, span(zx * 512, 512)]

    ex_second[0].wait_recv()
    ex_second[1].wait_recv()
    turn_extra(0, mine)
    ex_second[2].wait_recv()
    ex_second[3].wait_recv()
    turn_extra(1, other)
    send_t.wait_recv()
    for i in range(3):
        recv_q(i).wait_recv()

    for src in range(4):
        rcol[src] = jnp.broadcast_to(rgrad[src, 0:1, :], (128, 512)).T

    for k in range(1, 8):
        send_s(k).wait_recv()
    load_m.wait()
    eacc[...] = jnp.zeros_like(eacc)

    def reduce_copy(k, i, bufs, send, recv):
        src, dst, j = (bufs[0], bufs[1], i) if i < 2 else (bufs[2], bufs[3], i - 2)
        peer = below if i in (0, 2, 3) else above
        return to_rep(src.at[k, j], dst.at[k, j], send.at[k, i], recv.at[k, i], peer)

    def m_copy(k, i):
        return reduce_copy(k, i, (m1, m1r, m2, m2r), m_send, m_recv)

    def h_copy(k, i):
        return reduce_copy(k, i, (h1, h1r, h2, h2r), h_send, h_recv)

    def send_u(k):
        return to_rep(u.at[k, c], u.at[k, c], u_send.at[k], u_recv.at[k], sib)

    def send_hx(k):
        return to_rep(hx.at[k], hxr.at[k], h_send.at[k, 6], h_recv.at[k, 6], par)

    def mout_copy(k):
        cols = span(k * TILE, TILE)
        return pltpu.make_async_copy(mom.at[:, cols], mout_hbm.at[:, cols], mout_sem.at[k])

    grad_scale = inner_rate * D ** (-0.5) / N_REPLICA

    def stage(step, lag):
        k = step - lag
        return k, pl.when(jnp.logical_and(k >= 0, k < CHUNKS))

    @pl.loop(0, CHUNKS + LAGS[6])
    def _(step):
        k0, on0 = stage(step, LAGS[0])

        @on0
        def _():
            for group in range(2):
                hg_par(k0, group).wait_recv()
                hg_fwd(k0, group).start()

            @pl.when(k0 < CHUNKS - 3)
            def _():
                hg_par(k0 + 3, 0).start()
                hg_par(k0 + 3, 1).start()

        k1, on1 = stage(step, LAGS[1])

        @on1
        def _():
            m_copy(k1, 0).wait_recv()
            m2[k1, 0] = (cmid[k1, 0] + m1r[k1, 0].astype(F32)).astype(BF16)
            m_copy(k1, 2).start()
            m_copy(k1, 1).wait_recv()
            m2[k1, 3] = (cmid[k1, 1] + m1r[k1, 1].astype(F32)).astype(BF16)
            m_copy(k1, 5).start()

        k2, on2 = stage(step, LAGS[2])

        @on2
        def _():
            for i in range(2, 6):
                m_copy(k2, i).wait_recv()
            cols = span(k2 * TILE, TILE)
            for half, one, two in ((0, 0, 2), (1, 1, 3)):
                at = slice(half * 128, half * 128 + 128)
                pseudo = cown[k2, at] + (m2r[k2, one].astype(F32) + m2r[k2, two].astype(F32))
                new = outer_decay * mom[at, cols] + pseudo
                mom[at, cols] = new
                u[k2, c, at] = (outer_rate * (pseudo + outer_decay * new)).astype(BF16)
            send_u(k2).start()
            mout_copy(k2).start()

        @on0
        def _():
            for group in range(2):
                hg_sib(k0, group).wait_recv()
                hg_fwd_in(k0, group).wait_recv()
            for src in range(4):
                hgs[src] = (hg[k0, src].astype(F32) * jnp.tile(rcol[src], (1, 2))).astype(BF16)
            cc[...] = (
                jnp.dot(xt[...].reshape(1024, 2048), hgs[...].reshape(2048, TILE), preferred_element_type=F32)
                * grad_scale
            ).reshape(4, 256, TILE)
            m1[k0, 0] = cc[z_far, 0:128].astype(BF16)
            m_copy(k0, 0).start()
            m1[k0, 1] = cc[z_far, 128:256].astype(BF16)
            m_copy(k0, 1).start()
            m2[k0, 1] = cc[z_down, 128:256].astype(BF16)
            m_copy(k0, 3).start()
            m2[k0, 2] = cc[z_up, 0:128].astype(BF16)
            m_copy(k0, 4).start()
            cown[k0] = cc[z]
            cmid[k0, 0] = cc[z_down, 0:128]
            cmid[k0, 1] = cc[z_up, 128:256]

        k6, on6 = stage(step, LAGS[6])

        @on6
        def _():
            cols = span(k6 * TILE, TILE)
            base = jnp.dot(eg[...], w[:, cols], preferred_element_type=F32)
            send_hx(k6).wait_recv()
            moved = hown[k6, xh] + hxr[k6].astype(F32)
            after = (base - moved) * D ** (-0.5)
            v = after * sigmoid(after) * head_ref[0:1, cols]
            eacc[...] += v[:, :128] + v[:, 128:]

        k5, on5 = stage(step, LAGS[5])

        @on5
        def _():
            for i in range(2, 6):
                h_copy(k5, i).wait_recv()
            hown[k5, 0] += h2r[k5, 0].astype(F32) + h2r[k5, 2].astype(F32)
            hown[k5, 1] += h2r[k5, 1].astype(F32) + h2r[k5, 3].astype(F32)
            hx[k5] = hown[k5, 1 - xh].astype(BF16)
            send_hx(k5).start()

        k4, on4 = stage(step, LAGS[4])

        @on4
        def _():
            h_copy(k4, 0).wait_recv()
            h2[k4, 0] = (hc[k4, z_down * 2] + h1r[k4, 0].astype(F32)).astype(BF16)
            h_copy(k4, 2).start()
            h_copy(k4, 1).wait_recv()
            h2[k4, 3] = (hc[k4, z_up * 2 + 1] + h1r[k4, 1].astype(F32)).astype(BF16)
            h_copy(k4, 5).start()

        k3, on3 = stage(step, LAGS[3])

        @on3
        def _():
            send_u(k3).wait_recv()
            hc[k3] = jnp.dot(
                es[...].reshape(512, 512), u[k3].reshape(512, TILE), preferred_element_type=F32
            ).reshape(8, 64, TILE)
            h1[k3, 0] = hc[k3, z_far * 2].astype(BF16)
            h_copy(k3, 0).start()
            h1[k3, 1] = hc[k3, z_far * 2 + 1].astype(BF16)
            h_copy(k3, 1).start()
            h2[k3, 1] = hc[k3, z_down * 2 + 1].astype(BF16)
            h_copy(k3, 3).start()
            h2[k3, 2] = hc[k3, z_up * 2].astype(BF16)
            h_copy(k3, 4).start()
            hown[k3, 0] = hc[k3, z * 2]
            hown[k3, 1] = hc[k3, z * 2 + 1]

    def send_f(k):
        peer = (f + k) % 8
        return to_fsdp(eacc.at[span(peer * 8, 8), :], epart.at[f], f_send.at[k], f_recv.at[k], peer)

    for k in range(1, 8):
        send_f(k).start()
    epart[f] = eacc[span(f * 8, 8), :]

    @pl.loop(0, CHUNKS)
    def _(k):
        mout_copy(k).wait()
        for i in range(6):
            m_copy(k, i).wait_send()
            h_copy(k, i).wait_send()
        for group in range(2):
            hg_sib(k, group).wait_send()
            hg_par(k, group).wait_send()
            hg_fwd(k, group).wait_send()
        send_u(k).wait_send()
        send_hx(k).wait_send()

    for copy in main + extras + (send_t,) + tuple(over(core, i) for core, i in overs):
        copy.wait_send()
    for k in range(1, 8):
        send_e(k).wait_send()
        send_r(k).wait_send()
        send_s(k).wait_send()
    for i in range(3):
        send_q(i).wait_send()
    for k in range(1, 8):
        send_f(k).wait_recv()
    eval_ref[...] = jnp.sum(jnp.sum(epart[...], axis=0), axis=1, keepdims=True)
    for k in range(1, 8):
        send_f(k).wait_send()


def whole_round(weights, momentum, inputs, evals, head_scaled, pairs):
    vmem = pl.BlockSpec(memory_space=pltpu.VMEM)
    hbm = pl.BlockSpec(memory_space=pl.ANY)
    dma = pltpu.SemaphoreType.DMA
    return pl.pallas_call(
        round_kernel,
        out_shape=(jax.ShapeDtypeStruct((256, 1792), F32), jax.ShapeDtypeStruct((8, 1), F32)),
        in_specs=[hbm, hbm] + [vmem] * 4,
        out_specs=(hbm, vmem),
        scratch_shapes=[
            pltpu.VMEM((4096, 1792), BF16),
            pltpu.VMEM((256, 1792), F32),
            pltpu.VMEM((512, 4096), BF16),
            pltpu.VMEM((256, 128), F32),
            pltpu.VMEM((8, 8, 512), F32),
            pltpu.VMEM((4, 8, 512), F32),
            pltpu.VMEM((64, 4096), BF16),
            pltpu.VMEM((8, 64, 512), BF16),
            pltpu.VMEM((2, 4, 64, 256), BF16),
            pltpu.VMEM((8, 2, 4, 64, 256), BF16),
            pltpu.VMEM((4, 256, 2048), BF16),
            pltpu.VMEM((4, 256, 512), BF16),
            pltpu.VMEM((CHUNKS, 4, 512, TILE), BF16),
            pltpu.VMEM((4, 512, 128), F32),
            pltpu.VMEM((4, 512, TILE), BF16),
            pltpu.VMEM((4, 256, TILE), F32),
            pltpu.VMEM((CHUNKS, 256, TILE), F32),
            pltpu.VMEM((CHUNKS, 2, 128, TILE), F32),
            pltpu.VMEM((CHUNKS, 2, 128, TILE), BF16),
            pltpu.VMEM((CHUNKS, 2, 128, TILE), BF16),
            pltpu.VMEM((CHUNKS, 4, 128, TILE), BF16),
            pltpu.VMEM((CHUNKS, 4, 128, TILE), BF16),
            pltpu.VMEM((CHUNKS, 2, 256, TILE), BF16),
            pltpu.VMEM((CHUNKS, 8, 64, TILE), F32),
            pltpu.VMEM((CHUNKS, 2, 64, TILE), F32),
            pltpu.VMEM((CHUNKS, 2, 64, TILE), BF16),
            pltpu.VMEM((CHUNKS, 2, 64, TILE), BF16),
            pltpu.VMEM((CHUNKS, 4, 64, TILE), BF16),
            pltpu.VMEM((CHUNKS, 4, 64, TILE), BF16),
            pltpu.VMEM((CHUNKS, 64, TILE), BF16),
            pltpu.VMEM((CHUNKS, 64, TILE), BF16),
            pltpu.VMEM((64, 128), F32),
            pltpu.VMEM((8, 8, 128), F32),
            dma((2,)),
            dma((CHUNKS,)),
            dma((8,)), dma((8,)),
            dma((8,)), dma((8,)),
            dma((8,)), dma((8,)),
            dma((8,)), dma((8,)),
            dma((2, 2)), dma((2, 2)),
            dma((8,)), dma((8,)),
            dma, dma,
            dma((CHUNKS, 2, 3)), dma((CHUNKS, 2, 3)),
            dma((3,)), dma((3,)),
            dma((CHUNKS, 6)), dma((CHUNKS, 6)),
            dma((CHUNKS,)), dma((CHUNKS,)),
            dma((CHUNKS, 7)), dma((CHUNKS, 7)),
            dma((8,)), dma((8,)),
        ],
        compiler_params=pltpu.CompilerParams(collective_id=0, has_side_effects=True, vmem_limit_bytes=63 << 20),
    )(weights, momentum, inputs, evals, head_scaled, pairs.T)


def shards(weights, head_vector, momentum, batches, pair_index, eval_rows):
    head_scaled = head_vector * FF ** (-0.5)
    momentum_out, eval_rewards = whole_round(
        weights, momentum, batches[0], eval_rows, head_scaled[None, :], pair_index[0])
    return (momentum_out, eval_rewards[:, 0])


def solution(mesh):
    return jax.shard_map(
        shards,
        mesh=mesh,
        in_specs=(
            P(None, "fsdp"),
            P("fsdp"),
            P("replica", "fsdp"),
            P(None, ("replica", "fsdp"), None),
            P(None, "replica", None),
            P(("replica", "fsdp"), None),
        ),
        out_specs=(P("replica", "fsdp"), P(("replica", "fsdp"))),
        check_vma=False,
    )
```

```python
import jax
import jax.numpy as jnp
from jax import lax
from jax.experimental import pallas as pl
from jax.experimental.pallas import tpu as pltpu
from jax.sharding import PartitionSpec as P

D = 4096
FF = 14336
N_REPLICA = 16

inner_rate = 300.0
outer_rate = 0.7
outer_decay = 0.9
HIGH = lax.Precision.HIGHEST
F32 = jnp.float32
BF16 = jnp.bfloat16
MESH = pl.DeviceIdType.MESH
TILE = 256
CHUNKS = 7
AHEAD = 2
LAGS = (0, 1, 2, 3, 4, 5, 6)


def span(start, size):
    return pl.ds(pl.multiple_of(start, size), size)


def sigmoid(v):
    return 1.0 / (1.0 + jnp.exp(-v))


def round_kernel(
    w_hbm, mom_hbm, x_ref, e_ref, head_ref, pair_ref,
    mout_hbm, eval_ref,
    w, mom, xg, acc, rpart, rgrad, eg, es,
    eo, xe, xt, xts, hg, rcol, hgs, cc, cown, cmid, m1, m1r, m2, m2r, u, hc, hown, h1, h1r, h2, h2r, hx, hxr, eacc, epart,
    load_sem, mout_sem, x_send, x_recv, e_send, e_recv, r_send, r_recv, s_send, s_recv,
    o_send, o_recv, g_send, g_recv, t_send, t_recv, hg_send, hg_recv, q_send, q_recv, m_send, m_recv,
    u_send, u_recv, h_send, h_recv, f_send, f_recv,
):
    r = lax.axis_index("replica")
    f = lax.axis_index("fsdp")
    z, xh, c = r // 4, (r // 2) % 2, r % 2
    zx, q = z * 2 + xh, xh * 2 + c
    xl, y = f // 4, f % 4
    up, down = (y + 1) % 4, (y + 3) % 4
    mine, other = xl * 4, (1 - xl) * 4
    sib = z * 4 + xh * 2 + (1 - c)
    par = z * 4 + (1 - xh) * 2 + c
    z_up, z_down, z_far = (z + 1) % 4, (z + 3) % 4, (z + 2) % 4
    above, below = z_up * 4 + q, z_down * 4 + q

    def to_fsdp(src, dst, ss, rs, peer):
        return pltpu.make_async_remote_copy(
            src_ref=src, dst_ref=dst, send_sem=ss, recv_sem=rs, device_id={"fsdp": peer}, device_id_type=MESH)

    def to_rep(src, dst, ss, rs, peer):
        return pltpu.make_async_remote_copy(
            src_ref=src, dst_ref=dst, send_sem=ss, recv_sem=rs, device_id={"replica": peer}, device_id_type=MESH)

    load_w = pltpu.make_async_copy(w_hbm, w, load_sem.at[0])
    load_m = pltpu.make_async_copy(mom_hbm, mom, load_sem.at[1])
    load_w.start()
    load_m.start()

    barrier = pltpu.get_barrier_semaphore()
    for k in range(1, 8):
        pl.semaphore_signal(barrier, inc=1, device_id={"fsdp": (f + k) % 8}, device_id_type=MESH)
        pl.semaphore_signal(barrier, inc=1, device_id={"replica": ((zx + k) % 8) * 2 + c}, device_id_type=MESH)
    pl.semaphore_signal(barrier, inc=1, device_id={"replica": sib}, device_id_type=MESH)
    pl.semaphore_signal(
        barrier, inc=1, device_id={"replica": z * 4 + (1 - xh) * 2 + (1 - c)}, device_id_type=MESH)
    for core in range(2):
        pl.semaphore_signal(
            barrier, inc=1, device_id={"replica": z * 4 + (1 - xh) * 2 + core, "fsdp": other + y},
            device_id_type=MESH)

    xg[span(f * 64, 64), :] = x_ref[...]
    for core in range(2):
        for zp in range(4):
            eo[core, zp] = x_ref[:, span(zp * 1024 + ((1 - xh) * 2 + core) * 256, 256)]
    eg[span(f * 8, 8), :] = e_ref[...]
    pl.semaphore_wait(barrier, 18)

    def block(i, slot, peer, size=64, at=0):
        part = pl.ds(pl.multiple_of(slot * 64 + at, size), size)
        return to_fsdp(xg.at[part, :], xg.at[part, :], x_send.at[i], x_recv.at[i], peer)

    to_x = block(0, f, other + y)
    to_up = block(1, f, mine + up)
    to_down = block(2, f, mine + down)
    up_half = block(3, mine + down, mine + up, 32, 0)
    down_half = block(4, mine + up, mine + down, 32, 32)
    x_up = block(5, other + y, mine + up)
    x_down = block(6, other + y, mine + down)
    far_x = block(7, mine + (y + 2) % 4, other + y)
    main = (to_x, to_up, to_down, up_half, down_half, x_up, x_down, far_x)

    def extra(i, ref, peer):
        return to_fsdp(ref, ref, g_send.at[i], g_recv.at[i], peer)

    ex_first = (
        extra(0, xe.at[f], mine + up),
        extra(1, xe.at[f], mine + down),
        extra(2, xe.at[other + y], mine + up),
        extra(3, xe.at[other + y], mine + down),
    )
    ex_second = (
        extra(4, xe.at[mine + down, 0], mine + up),
        extra(5, xe.at[mine + up, 1], mine + down),
        extra(6, xe.at[other + down, 0], mine + up),
        extra(7, xe.at[other + up, 1], mine + down),
    )
    extras = ex_first + ex_second

    def over(core, i):
        return pltpu.make_async_remote_copy(
            src_ref=eo.at[core], dst_ref=xe.at[f, c], send_sem=o_send.at[core, i], recv_sem=o_recv.at[c, i],
            device_id={"replica": z * 4 + (1 - xh) * 2 + core, "fsdp": (mine if i == 0 else other) + y},
            device_id_type=MESH)

    def over_in(core, i):
        return pltpu.make_async_remote_copy(
            src_ref=eo.at[core], dst_ref=xe.at[(mine if i == 0 else other) + y, core], send_sem=o_send.at[core, i],
            recv_sem=o_recv.at[core, i],
            device_id={"replica": z * 4 + (1 - xh) * 2 + core, "fsdp": (mine if i == 0 else other) + y},
            device_id_type=MESH)

    overs = tuple((core, i) for core in range(2) for i in range(2))

    for copy in (to_x, to_up, to_down):
        copy.start()

    def send_e(k):
        return to_fsdp(e_ref, eg.at[span(f * 8, 8), :], e_send.at[k], e_recv.at[k], (f + k) % 8)

    to_up.wait_recv()
    up_half.start()
    to_down.wait_recv()
    down_half.start()
    to_x.wait_recv()
    for core, i in overs:
        over(core, i).start()
    up_half.wait_recv()
    down_half.wait_recv()
    far_x.start()
    x_up.start()
    x_down.start()

    load_w.wait()

    def hg_copy(k, group, i, src, dst, peer):
        at = slice(group * 256, group * 256 + 256)
        return to_rep(
            hg.at[k, src, at], hg.at[k, dst, at], hg_send.at[k, group, i], hg_recv.at[k, group, i], peer)

    def hg_sib(k, group):
        return hg_copy(k, group, 0, 0, 1, sib)

    def hg_par(k, group):
        return hg_copy(k, group, 1, 0, 2 + c, par)

    def hg_fwd(k, group):
        return hg_copy(k, group, 2, 2 + c, 2 + c, sib)

    def hg_fwd_in(k, group):
        return hg_copy(k, group, 2, 3 - c, 3 - c, sib)

    def forward(group, column):
        acc[...] = jnp.zeros_like(acc)

        @pl.loop(0, CHUNKS)
        def _(n):
            cols = span(n * TILE, TILE)
            h = jnp.dot(xg[span(column * 64, 256), :], w[:, cols], preferred_element_type=F32) * D ** (-0.5)
            hs = head_ref[0:1, cols] * FF ** (-0.5)
            sq = sigmoid(h)
            v = h * sq * hs
            acc[...] += v[:, :128] + v[:, 128:]
            hg[n, 0, group * 256 : group * 256 + 256, :] = (sq * (1.0 + h * (1.0 - sq)) * hs).astype(BF16)
            hg_sib(n, group).start()

            if group == 1:

                @pl.when(n < AHEAD)
                def _():
                    hg_par(n, group).start()

        ones = jnp.ones((8, 128), F32)
        return lax.dot_general(ones, acc[...], (((1,), (1,)), ((), ())), precision=HIGH, preferred_element_type=F32)

    def turn(group, column):
        @pl.loop(0, 4)
        def _(zp):
            at = slice(group * 256, group * 256 + 256)
            xt[zp, :, at] = xg[span(column * 64, 256), span(zp * 1024 + q * 256, 256)].T
            xts[zp, :, at] = xg[span(column * 64, 256), span(zp * 1024 + (xh * 2 + 1 - c) * 256, 256)].T

    def turn_extra(group, column):
        @pl.loop(0, 4)
        def _(zp):
            for core in range(2):
                at = slice(1024 + core * 512 + group * 256, 1024 + core * 512 + group * 256 + 256)
                xt[zp, :, at] = xe[pl.ds(column, 4), core, zp].reshape(256, 256).T

    first = forward(0, mine)
    turn(0, mine)
    x_up.wait_recv()
    x_down.wait_recv()
    far_x.wait_recv()
    for core, i in overs:
        over_in(core, i).wait_recv()
    for copy in ex_first:
        copy.start()

    @pl.loop(0, 2)
    def _(k):
        hg_par(k, 0).start()

    second = forward(1, other)
    low = xl == 0
    rpart[f] = jnp.concatenate([jnp.where(low, first, second), jnp.where(low, second, first)], axis=1)

    def send_r(k):
        return to_fsdp(rpart.at[f], rpart.at[f], r_send.at[k], r_recv.at[k], (f + k) % 8)

    for k in range(1, 8):
        send_r(k).start()
    ex_first[0].wait_recv()
    ex_second[0].start()
    ex_first[1].wait_recv()
    ex_second[1].start()
    ex_first[2].wait_recv()
    ex_second[2].start()
    ex_first[3].wait_recv()
    ex_second[3].start()
    turn(1, other)
    send_t = to_rep(xts, xt.at[:, :, 512:1024], t_send, t_recv, sib)
    send_t.start()

    for k in range(1, 8):
        send_r(k).wait_recv()
    rewards = jnp.sum(rpart[...], axis=0)
    at_row = lax.broadcasted_iota(jnp.int32, (512, 256), 0)
    turned = (pair_ref[1:2, :] == at_row).astype(F32) - (pair_ref[0:1, :] == at_row).astype(F32)
    weight = sigmoid(jnp.dot(rewards, turned, precision=HIGH, preferred_element_type=F32))
    grad = lax.dot_general(weight, turned, (((1,), (1,)), ((), ())), precision=HIGH, preferred_element_type=F32)
    rgrad[0] = jnp.where(low, grad, jnp.concatenate([grad[:, 256:], grad[:, :256]], axis=1))

    def send_q(i):
        peer = (sib, z * 4 + (1 - xh) * 2, z * 4 + (1 - xh) * 2 + 1)[i]
        return to_rep(rgrad.at[0], rgrad.at[1 if i == 0 else 2 + c], q_send.at[i], q_recv.at[0 if i == 0 else 1 + c], peer)

    def recv_q(i):
        return to_rep(rgrad.at[0], rgrad.at[1 + i], q_send.at[i], q_recv.at[i], sib)

    for i in range(3):
        send_q(i).start()

    hg_par(2, 0).start()
    hg_par(2, 1).start()

    def send_s(k):
        peer = (zx + k) % 8
        return to_rep(eg.at[:, span(peer * 512, 512)], es.at[zx], s_send.at[k], s_recv.at[k], peer * 2 + c)

    ex_second[0].wait_recv()
    ex_second[1].wait_recv()
    turn_extra(0, mine)
    ex_second[2].wait_recv()
    ex_second[3].wait_recv()
    for k in range(1, 8):
        send_e(k).start()
    turn_extra(1, other)
    send_t.wait_recv()
    for i in range(3):
        recv_q(i).wait_recv()

    for src in range(4):
        rcol[src] = jnp.broadcast_to(rgrad[src, 0:1, :], (128, 512)).T

    load_m.wait()
    eacc[...] = jnp.zeros_like(eacc)

    def reduce_copy(k, i, bufs, send, recv):
        src, dst, j = (bufs[0], bufs[1], i) if i < 2 else (bufs[2], bufs[3], i - 2)
        peer = below if i in (0, 2, 3) else above
        return to_rep(src.at[k, j], dst.at[k, j], send.at[k, i], recv.at[k, i], peer)

    def m_copy(k, i):
        return reduce_copy(k, i, (m1, m1r, m2, m2r), m_send, m_recv)

    def h_copy(k, i):
        return reduce_copy(k, i, (h1, h1r, h2, h2r), h_send, h_recv)

    def send_u(k):
        return to_rep(u.at[k, c], u.at[k, c], u_send.at[k], u_recv.at[k], sib)

    def send_hx(k):
        return to_rep(hx.at[k], hxr.at[k], h_send.at[k, 6], h_recv.at[k, 6], par)

    def mout_copy(k):
        cols = span(k * TILE, TILE)
        return pltpu.make_async_copy(mom.at[:, cols], mout_hbm.at[:, cols], mout_sem.at[k])

    grad_scale = inner_rate * D ** (-0.5) / N_REPLICA

    def stage(step, lag):
        k = step - lag
        return k, pl.when(jnp.logical_and(k >= 0, k < CHUNKS))

    @pl.loop(0, CHUNKS + LAGS[6])
    def _(step):
        k0, on0 = stage(step, LAGS[0])

        @on0
        def _():
            for group in range(2):
                hg_par(k0, group).wait_recv()
                hg_fwd(k0, group).start()

            @pl.when(k0 < CHUNKS - 3)
            def _():
                hg_par(k0 + 3, 0).start()
                hg_par(k0 + 3, 1).start()

        @on0
        def _():
            for group in range(2):
                hg_sib(k0, group).wait_recv()
                hg_fwd_in(k0, group).wait_recv()
            for src in range(4):
                hgs[src] = (hg[k0, src].astype(F32) * jnp.tile(rcol[src], (1, 2))).astype(BF16)
            cc[...] = (
                jnp.dot(xt[...].reshape(1024, 2048), hgs[...].reshape(2048, TILE), preferred_element_type=F32)
                * grad_scale
            ).reshape(4, 256, TILE)
            m1[k0, 0] = cc[z_far, 0:128].astype(BF16)
            m_copy(k0, 0).start()
            m1[k0, 1] = cc[z_far, 128:256].astype(BF16)
            m_copy(k0, 1).start()
            m2[k0, 1] = cc[z_down, 128:256].astype(BF16)
            m_copy(k0, 3).start()
            m2[k0, 2] = cc[z_up, 0:128].astype(BF16)
            m_copy(k0, 4).start()
            cown[k0] = cc[z]
            cmid[k0, 0] = cc[z_down, 0:128]
            cmid[k0, 1] = cc[z_up, 128:256]

        @pl.when(step == 1)
        def _():
            for k in range(1, 8):
                send_e(k).wait_recv()
            for k in range(1, 8):
                send_s(k).start()
            es[zx] = eg[:, span(zx * 512, 512)]

        @pl.when(step == 3)
        def _():
            for k in range(1, 8):
                send_s(k).wait_recv()

        k1, on1 = stage(step, LAGS[1])

        @on1
        def _():
            m_copy(k1, 0).wait_recv()
            m2[k1, 0] = (cmid[k1, 0] + m1r[k1, 0].astype(F32)).astype(BF16)
            m_copy(k1, 2).start()
            m_copy(k1, 1).wait_recv()
            m2[k1, 3] = (cmid[k1, 1] + m1r[k1, 1].astype(F32)).astype(BF16)
            m_copy(k1, 5).start()

        k2, on2 = stage(step, LAGS[2])

        @on2
        def _():
            for i in range(2, 6):
                m_copy(k2, i).wait_recv()
            cols = span(k2 * TILE, TILE)
            for half, one, two in ((0, 0, 2), (1, 1, 3)):
                at = slice(half * 128, half * 128 + 128)
                pseudo = cown[k2, at] + (m2r[k2, one].astype(F32) + m2r[k2, two].astype(F32))
                new = outer_decay * mom[at, cols] + pseudo
                mom[at, cols] = new
                u[k2, c, at] = (outer_rate * (pseudo + outer_decay * new)).astype(BF16)
            send_u(k2).start()
            mout_copy(k2).start()

        k6, on6 = stage(step, LAGS[6])

        @on6
        def _():
            cols = span(k6 * TILE, TILE)
            base = jnp.dot(eg[...], w[:, cols], preferred_element_type=F32)
            send_hx(k6).wait_recv()
            moved = hown[k6, xh] + hxr[k6].astype(F32)
            after = (base - moved) * D ** (-0.5)
            v = after * sigmoid(after) * (head_ref[0:1, cols] * FF ** (-0.5))
            eacc[...] += v[:, :128] + v[:, 128:]

        k5, on5 = stage(step, LAGS[5])

        @on5
        def _():
            for i in range(2, 6):
                h_copy(k5, i).wait_recv()
            hown[k5, 0] += h2r[k5, 0].astype(F32) + h2r[k5, 2].astype(F32)
            hown[k5, 1] += h2r[k5, 1].astype(F32) + h2r[k5, 3].astype(F32)
            hx[k5] = hown[k5, 1 - xh].astype(BF16)
            send_hx(k5).start()

        k4, on4 = stage(step, LAGS[4])

        @on4
        def _():
            h_copy(k4, 0).wait_recv()
            h2[k4, 0] = (hc[k4, z_down * 2] + h1r[k4, 0].astype(F32)).astype(BF16)
            h_copy(k4, 2).start()
            h_copy(k4, 1).wait_recv()
            h2[k4, 3] = (hc[k4, z_up * 2 + 1] + h1r[k4, 1].astype(F32)).astype(BF16)
            h_copy(k4, 5).start()

        k3, on3 = stage(step, LAGS[3])

        @on3
        def _():
            send_u(k3).wait_recv()
            hc[k3] = jnp.dot(
                es[...].reshape(512, 512), u[k3].reshape(512, TILE), preferred_element_type=F32
            ).reshape(8, 64, TILE)
            h1[k3, 0] = hc[k3, z_far * 2].astype(BF16)
            h_copy(k3, 0).start()
            h1[k3, 1] = hc[k3, z_far * 2 + 1].astype(BF16)
            h_copy(k3, 1).start()
            h2[k3, 1] = hc[k3, z_down * 2 + 1].astype(BF16)
            h_copy(k3, 3).start()
            h2[k3, 2] = hc[k3, z_up * 2].astype(BF16)
            h_copy(k3, 4).start()
            hown[k3, 0] = hc[k3, z * 2]
            hown[k3, 1] = hc[k3, z * 2 + 1]

    def send_f(k):
        peer = (f + k) % 8
        return to_fsdp(eacc.at[span(peer * 8, 8), :], epart.at[f], f_send.at[k], f_recv.at[k], peer)

    for k in range(1, 8):
        send_f(k).start()
    epart[f] = eacc[span(f * 8, 8), :]

    @pl.loop(0, CHUNKS)
    def _(k):
        mout_copy(k).wait()
        for i in range(6):
            m_copy(k, i).wait_send()
            h_copy(k, i).wait_send()
        for group in range(2):
            hg_sib(k, group).wait_send()
            hg_par(k, group).wait_send()
            hg_fwd(k, group).wait_send()
        send_u(k).wait_send()
        send_hx(k).wait_send()

    for copy in main + extras + (send_t,) + tuple(over(core, i) for core, i in overs):
        copy.wait_send()
    for k in range(1, 8):
        send_e(k).wait_send()
        send_r(k).wait_send()
        send_s(k).wait_send()
    for i in range(3):
        send_q(i).wait_send()
    for k in range(1, 8):
        send_f(k).wait_recv()
    ones = jnp.ones((8, 128), F32)
    eval_ref[...] = lax.dot_general(
        ones, jnp.sum(epart[...], axis=0), (((1,), (1,)), ((), ())), precision=HIGH, preferred_element_type=F32)[0:1]
    for k in range(1, 8):
        send_f(k).wait_send()


def whole_round(weights, momentum, inputs, evals, head, pairs):
    vmem = pl.BlockSpec(memory_space=pltpu.VMEM)
    hbm = pl.BlockSpec(memory_space=pl.ANY)
    dma = pltpu.SemaphoreType.DMA
    return pl.pallas_call(
        round_kernel,
        out_shape=(jax.ShapeDtypeStruct((256, 1792), F32), jax.ShapeDtypeStruct((1, 8), F32)),
        in_specs=[hbm, hbm] + [vmem] * 4,
        out_specs=(hbm, vmem),
        scratch_shapes=[
            pltpu.VMEM((4096, 1792), BF16),
            pltpu.VMEM((256, 1792), F32),
            pltpu.VMEM((512, 4096), BF16),
            pltpu.VMEM((256, 128), F32),
            pltpu.VMEM((8, 8, 512), F32),
            pltpu.VMEM((4, 8, 512), F32),
            pltpu.VMEM((64, 4096), BF16),
            pltpu.VMEM((8, 64, 512), BF16),
            pltpu.VMEM((2, 4, 64, 256), BF16),
            pltpu.VMEM((8, 2, 4, 64, 256), BF16),
            pltpu.VMEM((4, 256, 2048), BF16),
            pltpu.VMEM((4, 256, 512), BF16),
            pltpu.VMEM((CHUNKS, 4, 512, TILE), BF16),
            pltpu.VMEM((4, 512, 128), F32),
            pltpu.VMEM((4, 512, TILE), BF16),
            pltpu.VMEM((4, 256, TILE), F32),
            pltpu.VMEM((CHUNKS, 256, TILE), F32),
            pltpu.VMEM((CHUNKS, 2, 128, TILE), F32),
            pltpu.VMEM((CHUNKS, 2, 128, TILE), BF16),
            pltpu.VMEM((CHUNKS, 2, 128, TILE), BF16),
            pltpu.VMEM((CHUNKS, 4, 128, TILE), BF16),
            pltpu.VMEM((CHUNKS, 4, 128, TILE), BF16),
            pltpu.VMEM((CHUNKS, 2, 256, TILE), BF16),
            pltpu.VMEM((CHUNKS, 8, 64, TILE), F32),
            pltpu.VMEM((CHUNKS, 2, 64, TILE), F32),
            pltpu.VMEM((CHUNKS, 2, 64, TILE), BF16),
            pltpu.VMEM((CHUNKS, 2, 64, TILE), BF16),
            pltpu.VMEM((CHUNKS, 4, 64, TILE), BF16),
            pltpu.VMEM((CHUNKS, 4, 64, TILE), BF16),
            pltpu.VMEM((CHUNKS, 64, TILE), BF16),
            pltpu.VMEM((CHUNKS, 64, TILE), BF16),
            pltpu.VMEM((64, 128), F32),
            pltpu.VMEM((8, 8, 128), F32),
            dma((2,)),
            dma((CHUNKS,)),
            dma((8,)), dma((8,)),
            dma((8,)), dma((8,)),
            dma((8,)), dma((8,)),
            dma((8,)), dma((8,)),
            dma((2, 2)), dma((2, 2)),
            dma((8,)), dma((8,)),
            dma, dma,
            dma((CHUNKS, 2, 3)), dma((CHUNKS, 2, 3)),
            dma((3,)), dma((3,)),
            dma((CHUNKS, 6)), dma((CHUNKS, 6)),
            dma((CHUNKS,)), dma((CHUNKS,)),
            dma((CHUNKS, 7)), dma((CHUNKS, 7)),
            dma((8,)), dma((8,)),
        ],
        compiler_params=pltpu.CompilerParams(collective_id=0, has_side_effects=True, vmem_limit_bytes=63 << 20),
    )(weights, momentum, inputs, evals, head, pairs.T)


def shards(weights, head_vector, momentum, batches, pair_index, eval_rows):
    momentum_out, eval_rewards = whole_round(
        weights, momentum, batches[0], eval_rows, head_vector[None, :], pair_index[0])
    return (momentum_out, eval_rewards[0])


def solution(mesh):
    return jax.shard_map(
        shards,
        mesh=mesh,
        in_specs=(
            P(None, "fsdp"),
            P("fsdp"),
            P("replica", "fsdp"),
            P(None, ("replica", "fsdp"), None),
            P(None, "replica", None),
            P(("replica", "fsdp"), None),
        ),
        out_specs=(P("replica", "fsdp"), P(("replica", "fsdp"))),
        check_vma=False,
    )
```
